128 devices in a mesh: req: 8 (over x, core), tok: 16 (over z, y).
Axes of the slice: x: 4, y: 4, z: 4, core: 2. Of those that a mesh axis runs over, the one named last changes fastest.
Arguments:
- hidden: bfloat16 [8, 2048, 2048], P('req', 'tok'), may hold values from -4 to 4
- queries: bfloat16 [8, 2048, 3072], P('req', 'tok'), may hold values from -18 to 18
- fresh_latent: bfloat16 [8, 2048, 576], P('req', 'tok'), may hold values from -8 to 8
- latent_cache: bfloat16 [8, 16, 128, 576], P('req', 'tok'), may hold values from -8 to 8
- page_table: int32 [8, 16], P('req'), may hold values from 0 to 15, each once within a row
- cache_lengths: int32 [8], P('req'), may hold values from 2 to 2048, as said below
- routes: int32 [8, 2048, 6], P('req', 'tok'), may hold values from 0 to 63, all different within a row; in each aligned block of 128 rows (0 to 127, 128 to 255, ..., all dimensions but the last counted through in order) at most 14 rows name the same one
- route_gates: float32 [8, 2048, 6], P('req', 'tok'), may hold values from 0.05 to 0.45
- kv_up: bfloat16 [512, 4096], replicated, may hold values from -0.25 to 0.25
- out_proj: bfloat16 [2048, 2048], replicated, may hold values from -0.125 to 0.125
- latent_gain: float32 [512], replicated, may hold values from 0.1 to 1.9
- norm_gain: float32 [2048], replicated, may hold values from 0.1 to 1.9
- expert_in: bfloat16 [128, 2048, 1408], P(('req', 'tok')), may hold values from -0.125 to 0.125
- expert_out: bfloat16 [128, 704, 2048], P(('req', 'tok')), may hold values from -0.15625 to 0.15625
Outputs:
- layer_out: bfloat16 [8, 2048, 2048], P('req', 'tok')
- new_latent: bfloat16 [8, 2048, 576], P('req', 'tok')
The draws below stay inside these ranges and needn't reach their ends.
Inputs may be any that keep to these rules, and one draw needn't show every extreme that they name: `page_table`: each request's row names every pool page once. `cache_lengths`: some request has exactly 2048 cached tokens. `routes`: the 6 experts of a token differ; among the rows of one device no expert is named more than 14 times, and that bound is reached.
All inputs are finite; a program needn't handle non-finite values.
Results may differ from the reference program's by a relative error of at most 0.013.
Values may be sent and summed in bfloat16 or wider, within the bound.
A program may use at most 192 MiB of HBM per device.

```python
import math
import jax
import jax.numpy as jnp
import numpy as np
from jax import lax

D = 2048
H = 16
NOPE = 128
ROPE = 64
VD = 128
LAT = 512
EXPERTS = 64
FF_E = 1408
TOP = 6
TOK_DEV = 128
PAGE = 128
HALF = 704
CAP = 14
REQ = 8
NEW_TOK = 2048
POOL = 16
CTX_MAX = 2048
SLABS = 128
N_REQ = 8
N_TOK = 16


def request_lengths(key):
    first_key, second_key = jax.random.split(jax.random.fold_in(key, 7100))
    values = jax.random.randint(first_key, (REQ,), 2, CTX_MAX + 1)
    longest = jax.random.randint(second_key, (), 0, REQ)
    return jnp.where(jnp.arange(REQ) == longest, CTX_MAX, values).astype(jnp.int32)


def draw_cache_lengths(key, part):
    return request_lengths(key)


def background_values(key, shape):
    return jnp.clip(jax.random.normal(key, shape, jnp.float32), -6.0, 6.0)


def planted_pattern(key):
    sign_key, level_key = jax.random.split(jax.random.fold_in(key, 7001))
    half_rope = ROPE // 2
    pair_count = ROPE // 4
    column = jnp.arange(ROPE, dtype=jnp.int32)
    planted_column = column % half_rope >= half_rope - pair_count
    signs = (2 * jax.random.randint(sign_key, (REQ, ROPE), 0, 2) - 1).astype(jnp.float32)
    signs = jnp.where(column == half_rope - 1, 1.0, jnp.where(column == ROPE - 1, -1.0, signs))
    token = jnp.arange(NEW_TOK, dtype=jnp.int32)
    planted_row = token % 8 == 7
    levels = (8 + 2 * jax.random.randint(level_key, (REQ, NEW_TOK, H), 0, 3)).astype(jnp.float32)
    first_spot = (jnp.arange(REQ)[:, None, None] == 0) & (token[None, :, None] == 7) & (jnp.arange(H)[None, None, :] == 0)
    levels = jnp.where(first_spot, 12.0, levels)
    return (planted_column, signs, planted_row, levels)


def draw_fresh_latent(key, part):
    background = background_values(jax.random.fold_in(key, 7002), (REQ, NEW_TOK, LAT + ROPE))
    return background.astype(jnp.bfloat16)


def draw_latent_cache(key, part):
    planted_column, signs, planted_row, levels = planted_pattern(key)
    background = background_values(jax.random.fold_in(key, 7004), (REQ, POOL, PAGE, LAT + ROPE))
    row = jnp.arange(PAGE, dtype=jnp.int32)
    magnitude = jnp.where(row == 0, 8.0, jnp.where(row == 1, 7.9375, 0.0))
    picked = (row < 2)[:, None] & planted_column[None, :]
    planted = magnitude[None, None, :, None] * signs[:, None, None, :]
    rope_part = jnp.where(picked[None, None, :, :], planted, background[..., LAT:])
    return jnp.concatenate([background[..., :LAT], rope_part], axis=-1).astype(jnp.bfloat16)


def draw_queries(key, part):
    planted_column, signs, planted_row, levels = planted_pattern(key)
    lengths = request_lengths(key)
    background = background_values(jax.random.fold_in(key, 7003), (REQ, NEW_TOK, H, NOPE + ROPE))
    multiplier = max(1, 32 // ROPE)
    half_rope = ROPE // 2
    frequency = 10000.0 ** (-jnp.arange(half_rope, dtype=jnp.float32) * 2.0 / ROPE)
    positions = lengths[:, None] + jnp.arange(NEW_TOK, dtype=jnp.int32)[None, :]
    angles = positions.astype(jnp.float32)[:, :, None, None] * frequency[None, None, None, :]
    aligned = levels[..., None] * multiplier * signs[:, None, None, :]
    aligned = jnp.where(planted_column, aligned, 0.0)
    front_part = aligned[..., :half_rope]
    back_part = aligned[..., half_rope:]
    cosine = jnp.cos(angles)
    sine_part = jnp.sin(angles)
    turned = jnp.concatenate([front_part * cosine + back_part * sine_part, back_part * cosine - front_part * sine_part], axis=-1)
    row_mask = planted_row[None, :, None, None]
    rope_back = background[..., NOPE:]
    quiet = jnp.where(planted_column, 0.1 * rope_back, rope_back)
    rope_part = jnp.where(row_mask, turned, quiet)
    nope_part = jnp.where(row_mask, 0.0, background[..., :NOPE])
    joined = jnp.concatenate([nope_part, rope_part], axis=-1)
    return joined.reshape(REQ, NEW_TOK, H * (NOPE + ROPE)).astype(jnp.bfloat16)


def shard_levels(stream_key, extent, pieces, smallest, largest):
    def one(position, blocks):
        draws = jax.random.uniform(jax.random.fold_in(jax.random.fold_in(stream_key, 6), position), (blocks,), jnp.float32, smallest / len(pieces), largest / len(pieces))
        return jnp.repeat(jnp.exp(draws), extent[position] // blocks).reshape((-1,) + (1,) * (len(extent) - position - 1))

    level = one(*pieces[0])
    for cut in pieces[1:]:
        level = level * one(*cut)
    return level


def shared_out(stream_key, own, number, rows, amount, top, most, slope):
    order = jax.random.permutation(stream_key, amount)
    heavy_load, usual = shares(amount, rows * top, most, slope, True), shares(amount, rows * top, most, slope, False)
    places = jnp.arange(amount)

    def named(sizes, offset_by):
        used = int((sizes > 0).sum())
        fixed = max(1, used // 4)
        shifted = fixed + (places - fixed + offset_by * (used - fixed)) % max(1, amount - fixed)
        return jnp.zeros((amount,), jnp.int32).at[order[jnp.where(places < fixed, places, shifted)]].set(jnp.asarray(sizes, jnp.int32))

    sizes = jnp.where(number % 4 == 0, named(heavy_load, number // 4), named(usual, number - number // 4 - 1))
    mixed = jax.random.permutation(jax.random.fold_in(own, 3), amount)
    donor, receiver = mixed[0:amount // 2 * 2:2], mixed[1:amount // 2 * 2:2]
    margin = jnp.minimum(sizes[donor] - 1, most - sizes[receiver]) // 2
    margin = jnp.where((donor == order[0]) | (receiver == order[0]) | (sizes[receiver] == 0), 0, jnp.maximum(margin, 0))
    shifted = jax.random.randint(jax.random.fold_in(own, 4), (amount // 2,), 0, 1 << 20) % (margin + 1)
    sizes = sizes.at[donor].add(-shifted).at[receiver].add(shifted)
    items = jnp.searchsorted(jnp.cumsum(sizes), jnp.arange(rows * top), side="right").astype(jnp.int32)
    grid = items.reshape(top, rows).T
    grid = grid[jax.random.permutation(jax.random.fold_in(own, 1), rows)]
    offset_by = jax.random.randint(jax.random.fold_in(own, 2), (rows, 1), 0, top)
    return jnp.take_along_axis(grid, (jnp.arange(top)[None, :] + offset_by) % top, axis=1)


def shares(number_of, total, limit, skew, full):
    loads = [(1 << 20) // math.isqrt(grade ** skew) + 1 for grade in range(1, number_of + 1)]
    largest = limit if full else min(limit, max(-(-total // number_of), total * loads[0] // sum(loads)))
    least = 1 if total - largest >= number_of - 1 else 0
    counts, spare = [largest] + [least] * (number_of - 1), total - largest - least * (number_of - 1)
    while spare > 0:
        movable = [i for i in range(1, number_of) if counts[i] < largest] or [i for i in range(1, number_of) if counts[i] < limit]
        mass, left = sum([loads[i] for i in movable]), spare
        for i in movable:
            addition = min(limit - counts[i], max(1, left * loads[i] // mass), spare)
            counts[i] = counts[i] + addition
            spare = spare - addition
    return np.array(counts)


def centred(key, dims, deviation, bound, shards=(), held_as=jnp.bfloat16):
    entries = jax.random.normal(key, dims, jnp.float32) * deviation
    if len(shards) > 0:
        entries = shard_levels(key, dims, shards, -0.22, 0.18) * entries
    return jnp.clip(entries, min=-bound, max=bound).astype(held_as)


def setup_inputs(seed: int = 0) -> dict:
    key_of = jax.random.split(jax.random.key(seed), 15)
    hidden = centred(key_of[0], (REQ, NEW_TOK, D), 0.5, 4.0, ((0, 8), (1, 16)))
    queries = draw_queries(jax.random.fold_in(key_of[14], 71), 0)
    fresh_latent = draw_fresh_latent(jax.random.fold_in(key_of[14], 71), 0)
    latent_cache = draw_latent_cache(jax.random.fold_in(key_of[14], 71), 0)
    page_table = jax.vmap(lambda own: jax.random.permutation(own, POOL))(jax.random.split(key_of[4], REQ)).reshape((REQ, POOL)).astype(jnp.int32)
    cache_lengths = draw_cache_lengths(jax.random.fold_in(key_of[14], 71), 0)
    routes_keys = jax.random.split(jax.random.fold_in(key_of[6], 1), REQ * NEW_TOK // TOK_DEV)
    routes_turns = jax.random.permutation(jax.random.fold_in(key_of[6], 3), REQ * NEW_TOK // TOK_DEV)
    routes = jax.vmap(lambda own, number: shared_out(jax.random.fold_in(key_of[6], 2), own, number, TOK_DEV, EXPERTS, TOP, CAP, 2))(routes_keys, routes_turns).reshape((REQ, NEW_TOK, TOP))
    route_gates = jnp.clip(0.05 + 0.39999999 * jax.random.uniform(key_of[7], (REQ, NEW_TOK, TOP), jnp.float32) ** shard_levels(key_of[7], (REQ, NEW_TOK, TOP), ((0, 8), (1, 16)), -0.2, 0.2), 0.05, 0.45)
    kv_up = centred(key_of[8], (LAT, H * (NOPE + VD)), LAT ** -0.5, 0.25)
    out_proj = centred(key_of[9], (H * VD, D), (H * VD) ** -0.5, 0.125)
    latent_gain = jnp.clip(1.0 + 0.18 * jax.random.normal(key_of[10], (LAT,), jnp.float32), 0.1, 1.9)
    norm_gain = jnp.clip(1.0 + 0.18 * jax.random.normal(key_of[11], (D,), jnp.float32), 0.1, 1.9)
    expert_in = centred(key_of[12], (SLABS, D, 2 * HALF), D ** -0.5, 0.125, ((0, 128),))
    expert_out = centred(key_of[13], (SLABS, HALF, D), FF_E ** -0.5, 0.15625, ((0, 128),))
    return dict(hidden=hidden, queries=queries, fresh_latent=fresh_latent, latent_cache=latent_cache, page_table=page_table, cache_lengths=cache_lengths, routes=routes, route_gates=route_gates, kv_up=kv_up, out_proj=out_proj, latent_gain=latent_gain, norm_gain=norm_gain, expert_in=expert_in, expert_out=expert_out)


epsilon = 1e-06
theta_base = 10000.0

def rotary(values, angles):
    half_width = values.shape[-1] // 2
    front_part = values[..., :half_width]
    back_part = values[..., half_width:]
    cosine = jnp.cos(angles)
    sine_part = jnp.sin(angles)
    return jnp.concatenate([front_part * cosine - back_part * sine_part, back_part * cosine + front_part * sine_part], axis=-1)

def rms_scale(values, gain):
    return values * lax.rsqrt(lax.optimization_barrier(jnp.mean(values * values, axis=-1, keepdims=True)) + epsilon) * gain

def reference(hidden, queries, fresh_latent, latent_cache, page_table, cache_lengths, routes, route_gates, kv_up, out_proj, latent_gain, norm_gain, expert_in, expert_out):
    score_scale = 1.0 / math.sqrt(NOPE + ROPE)
    weights = kv_up.astype(jnp.float32).reshape(LAT, H, NOPE + VD)
    frequency = theta_base ** (-jnp.arange(ROPE // 2, dtype=jnp.float32) * 2.0 / ROPE)

    def request_attention(request):
        length = cache_lengths[request]
        positions = length + jnp.arange(NEW_TOK, dtype=jnp.int32)
        angles = positions.astype(jnp.float32)[:, None] * frequency[None, :]
        raw_latent = fresh_latent[request].astype(jnp.float32)
        latent = rms_scale(raw_latent[:, :LAT], latent_gain.astype(jnp.float32)).astype(jnp.bfloat16)
        key_rotated = rotary(raw_latent[:, LAT:], angles).astype(jnp.bfloat16)
        query_rows = queries[request].astype(jnp.float32).reshape(NEW_TOK, H, NOPE + ROPE)
        query_rotated = rotary(query_rows[:, :, NOPE:], angles[:, None, :]).astype(jnp.bfloat16)
        query_latent = jnp.einsum('thn,lhn->thl', query_rows[:, :, :NOPE], weights[:, :, :NOPE]).astype(jnp.bfloat16)
        pages = jnp.take(latent_cache[request], page_table[request], axis=0).reshape(CTX_MAX, LAT + ROPE)
        keys_latent = jnp.concatenate([pages[:, :LAT], latent], axis=0)
        keys_rotated = jnp.concatenate([pages[:, LAT:], key_rotated], axis=0)
        cache_positions = jnp.arange(CTX_MAX, dtype=jnp.int32)
        key_positions = jnp.concatenate([cache_positions, positions])
        key_valid = jnp.concatenate([cache_positions < length, jnp.ones((NEW_TOK,), dtype=bool)])
        allowed = key_valid[None, :] & (key_positions[None, :] <= positions[:, None])

        def one_head(head_index):
            head_query = jnp.take(query_latent, head_index, axis=1)
            head_rotated = jnp.take(query_rotated, head_index, axis=1)
            scores = jnp.dot(head_query, keys_latent.T, preferred_element_type=jnp.float32)
            scores = (scores + jnp.dot(head_rotated, keys_rotated.T, preferred_element_type=jnp.float32)) * score_scale
            scores = jnp.where(allowed, scores, -jnp.inf)
            highest = lax.optimization_barrier(jnp.max(scores, axis=1, keepdims=True))
            soft_weights = jnp.exp(scores - highest)
            totals = lax.optimization_barrier(jnp.sum(soft_weights, axis=1, keepdims=True))
            mixed = jnp.dot(soft_weights.astype(jnp.bfloat16), keys_latent, preferred_element_type=jnp.float32) / totals
            return mixed.astype(jnp.bfloat16)
        mixed_heads = lax.map(one_head, jnp.arange(H))
        head_out = jnp.einsum('htl,lhv->thv', mixed_heads.astype(jnp.float32), weights[:, :, NOPE:]).astype(jnp.bfloat16)
        attended = jnp.dot(head_out.reshape(NEW_TOK, H * VD), out_proj, preferred_element_type=jnp.float32)
        return (attended, jnp.concatenate([latent, key_rotated], axis=1))
    attended_all, new_latent = lax.map(request_attention, jnp.arange(REQ))
    residual = hidden.astype(jnp.float32) + attended_all
    normed = rms_scale(residual, norm_gain.astype(jnp.float32)).astype(jnp.bfloat16).reshape(REQ * NEW_TOK, D)
    flat_routes = routes.reshape(-1)
    flat_gates = route_gates.reshape(-1)
    token_of = jnp.arange(REQ * NEW_TOK * TOP, dtype=jnp.int32) // TOP
    most_rows = N_REQ * N_TOK * CAP

    def expert_step(carry, expert):
        named = flat_routes == expert
        chosen = jnp.nonzero(named, size=most_rows, fill_value=0)[0].astype(jnp.int32)
        live = jnp.arange(most_rows, dtype=jnp.int32) < jnp.sum(named.astype(jnp.int32))
        tokens_here = jnp.take(token_of, chosen)
        selected = jnp.take(normed, tokens_here, axis=0)
        gate_scale = jnp.where(live, jnp.take(flat_gates, chosen), 0.0)
        summed = jnp.zeros((most_rows, D), dtype=jnp.float32)
        for slab_half in range(2):
            slab_index = 2 * expert + slab_half
            projected = jnp.dot(selected, expert_in[slab_index], preferred_element_type=jnp.float32)
            active = (jax.nn.silu(projected[:, :HALF]) * projected[:, HALF:]).astype(jnp.bfloat16)
            slab_result = lax.optimization_barrier(jnp.dot(active, expert_out[slab_index], preferred_element_type=jnp.float32).astype(jnp.bfloat16))
            summed = summed + slab_result.astype(jnp.float32)
        carry = carry.at[tokens_here].add(gate_scale[:, None] * summed)
        return (carry, None)
    routed, unused = lax.scan(expert_step, jnp.zeros((REQ * NEW_TOK, D), dtype=jnp.float32), jnp.arange(EXPERTS, dtype=jnp.int32))
    layer_out = (residual + routed.reshape(REQ, NEW_TOK, D)).astype(jnp.bfloat16)
    return (layer_out, new_latent)
```

```python
import math

import jax
import jax.numpy as jnp
from jax import lax
from jax.experimental import pallas as pl
from jax.experimental.pallas import tpu as pltpu
from jax.sharding import PartitionSpec as P

H = 16
NOPE = 128
ROPE = 64
VD = 128
LAT = 512
EXPERTS = 64
SLOTS = 16
TOP = 6
BIG = 1 << 29

epsilon = 1e-06
theta_base = 10000.0
floor_score = -1e30
f32 = jnp.float32
bf16 = jnp.bfloat16


def rms_scale(values, gain):
    return values * lax.rsqrt(jnp.mean(values * values, axis=-1, keepdims=True) + epsilon) * gain


def turn(values, cosine, sine):
    half = values.shape[-1] // 2
    swapped = jnp.concatenate([values[:, half:], values[:, :half]], axis=-1)
    return values * cosine + swapped * sine


def dot(a, b):
    return jnp.dot(a, b, preferred_element_type=f32)


def dot_t(a, b):
    return lax.dot_general(a, b, (((1,), (1,)), ((), ())), preferred_element_type=f32)


def iota(shape, axis):
    return lax.broadcasted_iota(jnp.int32, shape, axis)


KB = 512
RB = 512


def attention_kernel(
    hidden, queries, cosine, sine, pages, fresh, krel, kv_up_hbm, out_proj_hbm, norm_gain, routes_t,
    residual_out, packed_out,
    kv_up, out_proj, ql, qr, acc, top, tot, heads, normed, packed, sems,
):
    rows = hidden.shape[0]
    first = lax.axis_index("tok") * rows
    load_up = pltpu.make_async_copy(kv_up_hbm, kv_up, sems.at[0])
    load_up.start()
    load_proj = pltpu.make_async_copy(out_proj_hbm, out_proj, sems.at[1])
    load_proj.start()
    width = NOPE + ROPE
    cos = cosine[...]
    sin = sine[...]
    for h in range(H):
        part = queries[:, h * width + NOPE : (h + 1) * width].astype(f32)
        qr[h * rows : (h + 1) * rows, :] = turn(part, cos, sin).astype(bf16)
    load_up.wait()
    for h in range(H):
        ql[h * rows : (h + 1) * rows, :] = dot_t(
            queries[:, h * width : h * width + NOPE], kv_up[:, h * 256 : h * 256 + NOPE]
        ).astype(bf16)
    top[...] = jnp.full_like(top, floor_score)
    tot[...] = jnp.zeros_like(tot)
    acc[...] = jnp.zeros_like(acc)
    scale = math.log2(math.e) / math.sqrt(width)
    qrel = first + lax.rem(iota((RB, KB), 0), rows)
    pages_per = KB // pages.shape[1]
    page_blocks = pages.shape[0] // pages_per

    def attend(keys_ref, block, rel_block):
        keys = keys_ref[pl.ds(block * pages_per, pages_per)].reshape(KB, LAT + ROPE)
        latent = keys[:, :LAT]
        rotated = keys[:, LAT:]
        allowed = krel[rel_block] <= qrel

        def scores(r):
            at = slice(r * RB, (r + 1) * RB)
            s = dot_t(ql[at, :], latent) + dot_t(qr[at, :], rotated)
            return jnp.where(allowed, s, floor_score)

        count = (H * rows) // RB
        current = scores(0)
        for r in range(count):
            following = scores(r + 1) if r + 1 < count else None
            at = slice(r * RB, (r + 1) * RB)
            before = top[at, :]
            now = jnp.maximum(before, jnp.max(current, axis=1, keepdims=True))
            fading = jnp.exp2((before - now) * scale)
            soft = jnp.exp2((current - jnp.tile(now, (1, KB // 128))) * scale)
            top[at, :] = now
            partial = soft[:, :128]
            for c in range(1, KB // 128):
                partial = partial + soft[:, c * 128 : (c + 1) * 128]
            tot[at, :] = tot[at, :] * fading + partial
            acc[at, :] = acc[at, :] * jnp.tile(fading, (1, LAT // 128)) + dot(soft.astype(bf16), latent)
            current = following

    def new_step(b, carry):
        attend(fresh, b, b)
        return carry

    def old_step(b, carry):
        attend(pages, b, b + page_blocks)
        return carry

    lax.fori_loop(0, page_blocks, new_step, 0)
    lax.fori_loop(0, page_blocks, old_step, 0)
    for h in range(H):
        at = slice(h * rows, (h + 1) * rows)
        total = jnp.sum(tot[at, :], axis=1, keepdims=True)
        mixed = (acc[at, :] / total).astype(bf16)
        heads[:, h * VD : (h + 1) * VD] = dot(
            mixed, kv_up[:, h * 256 + NOPE : (h + 1) * 256]
        ).astype(bf16)
    load_proj.wait()
    residual = hidden[...].astype(f32) + dot(heads[...], out_proj[...])
    residual_out[...] = residual
    normed[...] = rms_scale(residual, norm_gain[...]).astype(bf16)
    chosen = jnp.zeros((EXPERTS, rows), f32)
    for k in range(TOP):
        chosen = chosen + jnp.where(routes_t[k : k + 1, :] == iota((EXPERTS, rows), 0), 1.0, 0.0)
    earlier = jnp.where(iota((rows, rows), 0) < iota((rows, rows), 1), 1.0, 0.0).astype(bf16)
    rank = dot(chosen.astype(bf16), earlier)
    slot = jnp.where(chosen > 0.5, rank, -1.0)
    total_rows = EXPERTS * SLOTS
    spread = jnp.where(
        iota((total_rows, EXPERTS), 0) // SLOTS == iota((total_rows, EXPERTS), 1), 1.0, 0.0
    ).astype(bf16)
    slot_rows = dot(spread, slot.astype(bf16))
    wanted = lax.rem(iota((total_rows, rows), 0), SLOTS).astype(f32)
    placing = jnp.where(slot_rows == wanted, 1.0, 0.0).astype(bf16)
    packed[...] = dot(placing, normed[...]).astype(bf16).reshape(packed.shape)
    copies = [pltpu.make_async_copy(packed, packed_out.at[:, s], sems.at[s]) for s in range(2)]
    for copy in copies:
        copy.start()
    for copy in copies:
        copy.wait()


def expert_kernel(rows_ref, w_in, w_out, out_ref):
    half = w_out.shape[0]
    x = rows_ref[...].reshape(-1, rows_ref.shape[-1])
    g = dot(x, w_in[:, :half])
    u = dot(x, w_in[:, half:])
    active = (g / (1.0 + jnp.exp(-g)) * u).astype(bf16)
    out_ref[...] = dot(active, w_out[...]).astype(bf16).reshape(out_ref.shape)


def combine_kernel(returned, residual, routes, gates, out_ref, acc):
    step = pl.program_id(0)
    rows = residual.shape[0]
    group = returned.shape[0]
    width = group * SLOTS

    @pl.when(step == 0)
    def _():
        acc[...] = residual[...]

    expert = iota((rows, group), 1) + step * group
    chosen = jnp.zeros((rows, group), f32)
    gate = jnp.zeros((rows, group), f32)
    for k in range(TOP):
        hit = routes[:, k : k + 1] == expert
        chosen = chosen + jnp.where(hit, 1.0, 0.0)
        gate = gate + jnp.where(hit, gates[:, k : k + 1], 0.0)
    earlier = jnp.where(iota((rows, rows), 1) < iota((rows, rows), 0), 1.0, 0.0).astype(bf16)
    slot = jnp.where(chosen > 0.5, dot(earlier, chosen.astype(bf16)), -1.0)
    spread = jnp.where(
        iota((group, width), 1) // SLOTS == iota((group, width), 0), 1.0, 0.0
    ).astype(bf16)
    slot_cols = dot(slot.astype(bf16), spread)
    match = slot_cols == lax.rem(iota((rows, width), 1), SLOTS).astype(f32)
    high = gate.astype(bf16)
    low = (gate - high.astype(f32)).astype(bf16)
    weight_high = jnp.where(match, dot(high, spread), 0.0).astype(bf16)
    weight_low = jnp.where(match, dot(low, spread), 0.0).astype(bf16)
    total = acc[...]
    for s in range(2):
        block = returned[:, s].reshape(width, -1)
        total = total + dot(weight_high, block) + dot(weight_low, block)
    acc[...] = total

    @pl.when(step == pl.num_programs(0) - 1)
    def _():
        out_ref[...] = total.astype(bf16)


def local(
    hidden,
    queries,
    fresh_latent,
    latent_cache,
    page_table,
    cache_lengths,
    routes,
    route_gates,
    kv_up,
    out_proj,
    latent_gain,
    norm_gain,
    expert_in,
    expert_out,
):
    rows, width = hidden.shape[1:]
    pool = page_table.shape[1]
    page = latent_cache.shape[2]
    entry = latent_cache.shape[3]
    devices = lax.axis_size("req") * lax.axis_size("tok")
    length = cache_lengths[0]
    positions = length + lax.axis_index("tok") * rows + jnp.arange(rows, dtype=jnp.int32)
    frequency = theta_base ** (-jnp.arange(ROPE // 2, dtype=f32) * 2.0 / ROPE)
    angles = positions.astype(f32)[:, None] * frequency[None, :]
    cos = jnp.cos(angles)
    sin = jnp.sin(angles)
    cosine = jnp.concatenate([cos, cos], axis=1)
    sine = jnp.concatenate([-sin, sin], axis=1)
    raw = fresh_latent[0].astype(f32)
    latent = rms_scale(raw[:, :LAT], latent_gain).astype(bf16)
    key_rotated = turn(raw[:, LAT:], cosine, sine).astype(bf16)
    new_latent = jnp.concatenate([latent, key_rotated], axis=1)
    pages = lax.all_gather(latent_cache[0], "tok", axis=0, tiled=True)
    fresh = lax.all_gather(new_latent[None], "tok", axis=0, tiled=True)
    pool_index = jnp.arange(pool, dtype=jnp.int32)
    inverse = jnp.sum(
        jnp.where(page_table[0][None, :] == pool_index[:, None], pool_index[None, :], 0), axis=1
    )
    old_positions = (inverse[:, None] * page + jnp.arange(page, dtype=jnp.int32)[None, :]).reshape(-1)
    old_rel = jnp.where(old_positions < length, -1, BIG)
    krel = jnp.concatenate([jnp.arange(pool * rows, dtype=jnp.int32), old_rel]).reshape(-1, 1, KB)

    vmem = pl.BlockSpec(memory_space=pltpu.VMEM)
    anywhere = pl.BlockSpec(memory_space=pl.ANY)
    residual, packed = pl.pallas_call(
        attention_kernel,
        out_shape=(
            jax.ShapeDtypeStruct((rows, width), f32),
            jax.ShapeDtypeStruct((EXPERTS, 2, SLOTS, width), bf16),
        ),
        in_specs=[vmem] * 7 + [anywhere, anywhere, vmem, vmem],
        out_specs=(vmem, anywhere),
        scratch_shapes=[
            pltpu.VMEM(kv_up.shape, bf16),
            pltpu.VMEM(out_proj.shape, bf16),
            pltpu.VMEM((H * rows, LAT), bf16),
            pltpu.VMEM((H * rows, ROPE), bf16),
            pltpu.VMEM((H * rows, LAT), f32),
            pltpu.VMEM((H * rows, 128), f32),
            pltpu.VMEM((H * rows, 128), f32),
            pltpu.VMEM((rows, H * VD), bf16),
            pltpu.VMEM((rows, width), bf16),
            pltpu.VMEM((EXPERTS, SLOTS, width), bf16),
            pltpu.SemaphoreType.DMA((2,)),
        ],
        compiler_params=pltpu.CompilerParams(vmem_limit_bytes=60 << 20),
        name="attention",
    )(
        hidden[0], queries[0], cosine, sine, pages, fresh, krel, kv_up, out_proj,
        norm_gain[None], routes[0].T,
    )
    sent = packed.reshape(devices, SLOTS, width)
    arrived = lax.all_to_all(sent, ("req", "tok"), split_axis=0, concat_axis=0, tiled=True)
    steps = 8
    block = pl.BlockSpec((devices // steps, SLOTS, width), lambda i: (i, 0, 0))
    results = pl.pallas_call(
        expert_kernel,
        out_shape=jax.ShapeDtypeStruct((devices, SLOTS, width), bf16),
        grid=(steps,),
        in_specs=[
            block,
            pl.BlockSpec(expert_in.shape[1:], lambda i: (0, 0), pipeline_mode=pl.Buffered(1)),
            pl.BlockSpec(expert_out.shape[1:], lambda i: (0, 0), pipeline_mode=pl.Buffered(1)),
        ],
        out_specs=block,
        compiler_params=pltpu.CompilerParams(vmem_limit_bytes=60 << 20),
        name="experts",
    )(arrived, expert_in[0], expert_out[0])
    returned = lax.all_to_all(results, ("req", "tok"), split_axis=0, concat_axis=0, tiled=True)
    groups = 4
    layer_out = pl.pallas_call(
        combine_kernel,
        out_shape=jax.ShapeDtypeStruct((rows, width), bf16),
        grid=(groups,),
        in_specs=[
            pl.BlockSpec((EXPERTS // groups, 2, SLOTS, width), lambda i: (i, 0, 0, 0)),
            pl.BlockSpec((rows, width), lambda i: (0, 0)),
            pl.BlockSpec((rows, TOP), lambda i: (0, 0)),
            pl.BlockSpec((rows, TOP), lambda i: (0, 0)),
        ],
        out_specs=pl.BlockSpec((rows, width), lambda i: (0, 0)),
        scratch_shapes=[pltpu.VMEM((rows, width), f32)],
        compiler_params=pltpu.CompilerParams(vmem_limit_bytes=60 << 20),
        name="combine",
    )(returned.reshape(EXPERTS, 2, SLOTS, width), residual, routes[0], route_gates[0])
    return (layer_out[None], new_latent[None])


def solution(mesh):
    placed = (
        P("req", "tok", None),
        P("req", "tok", None),
        P("req", "tok", None),
        P("req", "tok", None, None),
        P("req", None),
        P("req"),
        P("req", "tok", None),
        P("req", "tok", None),
        P(),
        P(),
        P(),
        P(),
        P(("req", "tok"), None, None),
        P(("req", "tok"), None, None),
    )
    return jax.shard_map(
        local,
        mesh=mesh,
        in_specs=placed,
        out_specs=(P("req", "tok", None), P("req", "tok", None)),
        check_vma=False,
    )
```

```python
import math

import jax
import jax.numpy as jnp
from jax import lax
from jax.experimental import pallas as pl
from jax.experimental.pallas import tpu as pltpu
from jax.sharding import PartitionSpec as P

H = 16
NOPE = 128
ROPE = 64
VD = 128
LAT = 512
EXPERTS = 64
SLOTS = 16
TOP = 6
BIG = 1 << 29

epsilon = 1e-06
theta_base = 10000.0
floor_score = -1e30
f32 = jnp.float32
bf16 = jnp.bfloat16


def rms_scale(values, gain):
    return values * lax.rsqrt(jnp.mean(values * values, axis=-1, keepdims=True) + epsilon) * gain


def turn(values, cosine, sine):
    half = values.shape[-1] // 2
    swapped = jnp.concatenate([values[:, half:], values[:, :half]], axis=-1)
    return values * cosine + swapped * sine


def dot(a, b):
    return jnp.dot(a, b, preferred_element_type=f32)


def dot_t(a, b):
    return lax.dot_general(a, b, (((1,), (1,)), ((), ())), preferred_element_type=f32)


def iota(shape, axis):
    return lax.broadcasted_iota(jnp.int32, shape, axis)


KB = 256
RB = 512
SIDE = 4
MOVES = 36
ENTRY = 2 * (LAT + ROPE)


def pick(step, values):
    chosen = values[0]
    for n in range(1, len(values)):
        chosen = jnp.where(step == n, values[n], chosen)
    return chosen


def attention_kernel(
    hidden, queries, cosine, sine, own, old_rel, kv_up_hbm, out_proj_hbm, norm_gain, routes_t,
    residual_out, packed_out,
    kv, kv_up, out_proj, ql, qr_old, qr_new, acc, top, tot, heads, normed, packed,
    sems, send_sems, recv_sems,
):
    rows = hidden.shape[0]
    me = lax.axis_index("tok")
    my_z = me // SIDE
    my_y = lax.rem(me, SIDE)
    first = me * rows

    def at_offset(dy, dz):
        return lax.rem(my_z + dz + SIDE, SIDE) * SIDE + lax.rem(my_y + dy + SIDE, SIDE)

    def offset(axis, sign):
        return (sign, 0) if axis == "y" else (0, sign)

    directions = [("y", 1), ("y", -1), ("z", 1), ("z", -1)]
    load_up = pltpu.make_async_copy(kv_up_hbm, kv_up, sems.at[0])
    load_up.start()
    load_proj = pltpu.make_async_copy(out_proj_hbm, out_proj, sems.at[1])
    load_proj.start()
    keep = pltpu.make_async_copy(own, kv.at[me], sems.at[2])
    keep.start()

    barrier = pltpu.get_barrier_semaphore()
    for axis, sign in directions:
        pl.semaphore_signal(
            barrier,
            inc=1,
            device_id={"tok": at_offset(*offset(axis, sign))},
            device_id_type=pl.DeviceIdType.MESH,
        )
    pl.semaphore_wait(barrier, len(directions))

    def move(number, source, block, row, count, axis, sign):
        target = at_offset(*offset(axis, sign))
        return pltpu.make_async_remote_copy(
            src_ref=source.at[pl.ds(row, count)],
            dst_ref=kv.at[block, pl.ds(row, count)],
            send_sem=send_sems.at[number],
            recv_sem=recv_sems.at[number],
            device_id={"tok": target},
            device_id_type=pl.DeviceIdType.MESH,
        )

    quarter = rows // 4
    plans = [[], [], [], []]
    for axis, sign in directions:
        plans[0].append((None, 0, rows, axis, sign))
    for axis, sign in directions:
        back = offset(axis, -sign)
        start = 0 if sign > 0 else quarter
        plans[1].append((back, start, quarter, axis, sign))
        plans[1].append((back, start + 2 * quarter, quarter, axis, sign))
        for other in (1, -1):
            side = (other, 0) if axis == "z" else (0, other)
            plans[1].append((side, 0 if axis == "z" else 2 * quarter, 2 * quarter, axis, sign))
    for axis, sign in directions:
        far = (2, 0) if axis == "z" else (0, 2)
        half = 0 if axis == "z" else 2 * quarter
        start = half + (0 if sign > 0 else quarter)
        plans[2].append((far, half, 2 * quarter, axis, sign))
        for other in (1, -1):
            corner = (other, -sign) if axis == "z" else (-sign, other)
            plans[2].append((corner, start, quarter, axis, sign))
        corner = (2, -sign) if axis == "z" else (-sign, 2)
        plans[3].append((corner, start, quarter, axis, sign))

    first_number = [0]
    for plan in plans:
        first_number.append(first_number[-1] + len(plan))

    def copies(level):
        made = []
        for n, (source, row, count, axis, sign) in enumerate(plans[level]):
            if source is None:
                block, ref = me, own
            else:
                block = at_offset(*source)
                ref = kv.at[block]
            made.append(move(first_number[level] + n, ref, block, row, count, axis, sign))
        return made

    def start_level(level):
        for copy in copies(level):
            copy.start()

    def finish_level(level):
        for copy in copies(level):
            copy.wait()

    start_level(0)
    width = NOPE + ROPE
    cos = cosine[...]
    sin = sine[...]
    blank = jnp.zeros((rows, ROPE), bf16)
    for h in range(H):
        at = slice(h * rows, (h + 1) * rows)
        part = queries[:, h * width + NOPE : (h + 1) * width].astype(f32)
        turned = turn(part, cos, sin).astype(bf16)
        qr_old[at, :] = jnp.concatenate([turned, blank], axis=1)
        qr_new[at, :] = jnp.concatenate([blank, turned], axis=1)
    load_up.wait()
    for h in range(H):
        ql[h * rows : (h + 1) * rows, :] = dot_t(
            queries[:, h * width : h * width + NOPE], kv_up[:, h * 256 : h * 256 + NOPE]
        ).astype(bf16)
    top[...] = jnp.full_like(top, floor_score)
    tot[...] = jnp.zeros_like(tot)
    acc[...] = jnp.zeros_like(acc)
    scale = math.log2(math.e) / math.sqrt(width)
    qrel = first + lax.rem(iota((RB, KB), 0), rows)
    keep.wait()

    order = [
        (0, 0),
        (1, 0), (-1, 0), (0, 1), (0, -1),
        (2, 0), (0, 2), (1, 1), (1, -1), (-1, 1), (-1, -1),
        (2, 1), (2, -1), (1, 2), (-1, 2),
        (2, 2),
    ]
    pairs = len(order) // 2
    level_at = {0: 0, 2: 1, 5: 2, 7: 3}

    def attend(step, carry):
        for when, level in level_at.items():

            @pl.when(step == when)
            def _():
                finish_level(level)
                if level + 1 < len(plans):
                    start_level(level + 1)

        one = pick(step, [at_offset(*order[2 * n]) for n in range(pairs)])
        two = pick(step, [at_offset(*order[2 * n + 1]) for n in range(pairs)])
        old = jnp.concatenate([kv[one, :, :LAT], kv[two, :, :LAT]], axis=0)
        new = jnp.concatenate([kv[one, :, LAT : 2 * LAT], kv[two, :, LAT : 2 * LAT]], axis=0)
        rotated = jnp.concatenate([kv[one, :, 2 * LAT :], kv[two, :, 2 * LAT :]], axis=0)
        old_at = jnp.concatenate([old_rel[one], old_rel[two]], axis=1)
        lane = iota((1, rows), 1)
        new_at = jnp.concatenate([one * rows + lane, two * rows + lane], axis=1)
        old_allowed = old_at <= qrel
        new_allowed = new_at <= qrel

        def scores(r):
            at = slice(r * RB, (r + 1) * RB)
            s_old = dot_t(ql[at, :], old) + dot_t(qr_old[at, :], rotated)
            s_new = dot_t(ql[at, :], new) + dot_t(qr_new[at, :], rotated)
            return (
                jnp.where(old_allowed, s_old, floor_score),
                jnp.where(new_allowed, s_new, floor_score),
            )

        count = (H * rows) // RB
        current = scores(0)
        for r in range(count):
            following = scores(r + 1) if r + 1 < count else None
            at = slice(r * RB, (r + 1) * RB)
            before = top[at, :]
            s_old, s_new = current
            now = jnp.maximum(before, jnp.max(jnp.maximum(s_old, s_new), axis=1, keepdims=True))
            fading = jnp.exp2((before - now) * scale)
            wide = jnp.tile(now, (1, KB // 128))
            soft_old = jnp.exp2((s_old - wide) * scale)
            soft_new = jnp.exp2((s_new - wide) * scale)
            top[at, :] = now
            both = soft_old + soft_new
            tot[at, :] = tot[at, :] * fading + both[:, :128] + both[:, 128:]
            acc[at, :] = (
                acc[at, :] * jnp.tile(fading, (1, LAT // 128))
                + dot(soft_old.astype(bf16), old)
                + dot(soft_new.astype(bf16), new)
            )
            current = following
        return carry

    lax.fori_loop(0, pairs, attend, 0)
    for h in range(H):
        at = slice(h * rows, (h + 1) * rows)
        total = jnp.sum(tot[at, :], axis=1, keepdims=True)
        mixed = (acc[at, :] / total).astype(bf16)
        heads[:, h * VD : (h + 1) * VD] = dot(
            mixed, kv_up[:, h * 256 + NOPE : (h + 1) * 256]
        ).astype(bf16)
    load_proj.wait()
    residual = hidden[...].astype(f32) + dot(heads[...], out_proj[...])
    residual_out[...] = residual
    normed[...] = rms_scale(residual, norm_gain[...]).astype(bf16)
    chosen = jnp.zeros((EXPERTS, rows), f32)
    for k in range(TOP):
        chosen = chosen + jnp.where(routes_t[k : k + 1, :] == iota((EXPERTS, rows), 0), 1.0, 0.0)
    earlier = jnp.where(iota((rows, rows), 0) < iota((rows, rows), 1), 1.0, 0.0).astype(bf16)
    rank = dot(chosen.astype(bf16), earlier)
    slot = jnp.where(chosen > 0.5, rank, -1.0)
    total_rows = EXPERTS * SLOTS
    spread = jnp.where(
        iota((total_rows, EXPERTS), 0) // SLOTS == iota((total_rows, EXPERTS), 1), 1.0, 0.0
    ).astype(bf16)
    slot_rows = dot(spread, slot.astype(bf16))
    wanted = lax.rem(iota((total_rows, rows), 0), SLOTS).astype(f32)
    placing = jnp.where(slot_rows == wanted, 1.0, 0.0).astype(bf16)
    packed[...] = dot(placing, normed[...]).astype(bf16).reshape(packed.shape)
    outgoing = [pltpu.make_async_copy(packed, packed_out.at[:, s], sems.at[s]) for s in range(2)]
    for copy in outgoing:
        copy.start()
    for copy in outgoing:
        copy.wait()


def expert_kernel(rows_ref, w_in, w_out, out_ref):
    half = w_out.shape[0]
    x = rows_ref[...].reshape(-1, rows_ref.shape[-1])
    g = dot(x, w_in[:, :half])
    u = dot(x, w_in[:, half:])
    active = (g / (1.0 + jnp.exp(-g)) * u).astype(bf16)
    out_ref[...] = dot(active, w_out[...]).astype(bf16).reshape(out_ref.shape)


def combine_kernel(returned, residual, routes, gates, out_ref, acc):
    step = pl.program_id(0)
    rows = residual.shape[0]
    group = returned.shape[0]
    width = group * SLOTS

    @pl.when(step == 0)
    def _():
        acc[...] = residual[...]

    expert = iota((rows, group), 1) + step * group
    chosen = jnp.zeros((rows, group), f32)
    gate = jnp.zeros((rows, group), f32)
    for k in range(TOP):
        hit = routes[:, k : k + 1] == expert
        chosen = chosen + jnp.where(hit, 1.0, 0.0)
        gate = gate + jnp.where(hit, gates[:, k : k + 1], 0.0)
    earlier = jnp.where(iota((rows, rows), 1) < iota((rows, rows), 0), 1.0, 0.0).astype(bf16)
    slot = jnp.where(chosen > 0.5, dot(earlier, chosen.astype(bf16)), -1.0)
    spread = jnp.where(
        iota((group, width), 1) // SLOTS == iota((group, width), 0), 1.0, 0.0
    ).astype(bf16)
    slot_cols = dot(slot.astype(bf16), spread)
    match = slot_cols == lax.rem(iota((rows, width), 1), SLOTS).astype(f32)
    high = gate.astype(bf16)
    low = (gate - high.astype(f32)).astype(bf16)
    weight_high = jnp.where(match, dot(high, spread), 0.0).astype(bf16)
    weight_low = jnp.where(match, dot(low, spread), 0.0).astype(bf16)
    total = acc[...]
    for s in range(2):
        block = returned[:, s].reshape(width, -1)
        total = total + dot(weight_high, block) + dot(weight_low, block)
    acc[...] = total

    @pl.when(step == pl.num_programs(0) - 1)
    def _():
        out_ref[...] = total.astype(bf16)


def local(
    hidden,
    queries,
    fresh_latent,
    latent_cache,
    page_table,
    cache_lengths,
    routes,
    route_gates,
    kv_up,
    out_proj,
    latent_gain,
    norm_gain,
    expert_in,
    expert_out,
):
    rows, width = hidden.shape[1:]
    pool = page_table.shape[1]
    page = latent_cache.shape[2]
    devices = lax.axis_size("req") * lax.axis_size("tok")
    length = cache_lengths[0]
    positions = length + lax.axis_index("tok") * rows + jnp.arange(rows, dtype=jnp.int32)
    frequency = theta_base ** (-jnp.arange(ROPE // 2, dtype=f32) * 2.0 / ROPE)
    angles = positions.astype(f32)[:, None] * frequency[None, :]
    cos = jnp.cos(angles)
    sin = jnp.sin(angles)
    cosine = jnp.concatenate([cos, cos], axis=1)
    sine = jnp.concatenate([-sin, sin], axis=1)
    raw = fresh_latent[0].astype(f32)
    latent = rms_scale(raw[:, :LAT], latent_gain).astype(bf16)
    key_rotated = turn(raw[:, LAT:], cosine, sine).astype(bf16)
    new_latent = jnp.concatenate([latent, key_rotated], axis=1)
    cached = latent_cache[0, 0]
    own = jnp.concatenate([cached[:, :LAT], latent, cached[:, LAT:], key_rotated], axis=1)
    pool_index = jnp.arange(pool, dtype=jnp.int32)
    inverse = jnp.sum(
        jnp.where(page_table[0][None, :] == pool_index[:, None], pool_index[None, :], 0), axis=1
    )
    old_positions = inverse[:, None] * page + jnp.arange(page, dtype=jnp.int32)[None, :]
    old_rel = jnp.where(old_positions < length, -1, BIG)[:, None, :]

    vmem = pl.BlockSpec(memory_space=pltpu.VMEM)
    anywhere = pl.BlockSpec(memory_space=pl.ANY)
    residual, packed = pl.pallas_call(
        attention_kernel,
        out_shape=(
            jax.ShapeDtypeStruct((rows, width), f32),
            jax.ShapeDtypeStruct((EXPERTS, 2, SLOTS, width), bf16),
        ),
        in_specs=[vmem] * 6 + [anywhere, anywhere, vmem, vmem],
        out_specs=(vmem, anywhere),
        scratch_shapes=[
            pltpu.VMEM((pool, rows, ENTRY), bf16),
            pltpu.VMEM(kv_up.shape, bf16),
            pltpu.VMEM(out_proj.shape, bf16),
            pltpu.VMEM((H * rows, LAT), bf16),
            pltpu.VMEM((H * rows, 2 * ROPE), bf16),
            pltpu.VMEM((H * rows, 2 * ROPE), bf16),
            pltpu.VMEM((H * rows, LAT), f32),
            pltpu.VMEM((H * rows, 128), f32),
            pltpu.VMEM((H * rows, 128), f32),
            pltpu.VMEM((rows, H * VD), bf16),
            pltpu.VMEM((rows, width), bf16),
            pltpu.VMEM((EXPERTS, SLOTS, width), bf16),
            pltpu.SemaphoreType.DMA((3,)),
            pltpu.SemaphoreType.DMA((MOVES,)),
            pltpu.SemaphoreType.DMA((MOVES,)),
        ],
        compiler_params=pltpu.CompilerParams(
            vmem_limit_bytes=60 << 20, collective_id=0, has_side_effects=True
        ),
        name="attention",
    )(
        hidden[0], queries[0], cosine, sine, own, old_rel, kv_up, out_proj,
        norm_gain[None], routes[0].T,
    )
    sent = packed.reshape(devices, SLOTS, width)
    arrived = lax.all_to_all(sent, ("req", "tok"), split_axis=0, concat_axis=0, tiled=True)
    steps = 8
    block = pl.BlockSpec((devices // steps, SLOTS, width), lambda i: (i, 0, 0))
    results = pl.pallas_call(
        expert_kernel,
        out_shape=jax.ShapeDtypeStruct((devices, SLOTS, width), bf16),
        grid=(steps,),
        in_specs=[
            block,
            pl.BlockSpec(expert_in.shape[1:], lambda i: (0, 0), pipeline_mode=pl.Buffered(1)),
            pl.BlockSpec(expert_out.shape[1:], lambda i: (0, 0), pipeline_mode=pl.Buffered(1)),
        ],
        out_specs=block,
        compiler_params=pltpu.CompilerParams(vmem_limit_bytes=60 << 20),
        name="experts",
    )(arrived, expert_in[0], expert_out[0])
    returned = lax.all_to_all(results, ("req", "tok"), split_axis=0, concat_axis=0, tiled=True)
    groups = 4
    layer_out = pl.pallas_call(
        combine_kernel,
        out_shape=jax.ShapeDtypeStruct((rows, width), bf16),
        grid=(groups,),
        in_specs=[
            pl.BlockSpec((EXPERTS // groups, 2, SLOTS, width), lambda i: (i, 0, 0, 0)),
            pl.BlockSpec((rows, width), lambda i: (0, 0)),
            pl.BlockSpec((rows, TOP), lambda i: (0, 0)),
            pl.BlockSpec((rows, TOP), lambda i: (0, 0)),
        ],
        out_specs=pl.BlockSpec((rows, width), lambda i: (0, 0)),
        scratch_shapes=[pltpu.VMEM((rows, width), f32)],
        compiler_params=pltpu.CompilerParams(vmem_limit_bytes=60 << 20),
        name="combine",
    )(returned.reshape(EXPERTS, 2, SLOTS, width), residual, routes[0], route_gates[0])
    return (layer_out[None], new_latent[None])


def solution(mesh):
    placed = (
        P("req", "tok", None),
        P("req", "tok", None),
        P("req", "tok", None),
        P("req", "tok", None, None),
        P("req", None),
        P("req"),
        P("req", "tok", None),
        P("req", "tok", None),
        P(),
        P(),
        P(),
        P(),
        P(("req", "tok"), None, None),
        P(("req", "tok"), None, None),
    )
    return jax.shard_map(
        local,
        mesh=mesh,
        in_specs=placed,
        out_specs=(P("req", "tok", None), P("req", "tok", None)),
        check_vma=False,
    )
```
